32 devices in a mesh: row: 4 (over x, core), col: 8 (over z, y).
Axes of the slice: x: 2, y: 2, z: 4, core: 2. Of those that a mesh axis runs over, the one named last changes fastest.
Arguments:
- vectors: float32 [8192, 1024], P('row', 'col'), may hold values from -6 to 6
- reflectors: float32 [4, 32, 256, 128], P('row', 'col'), may hold values from -0.375 to 0.375
- wy_factors: float32 [4, 32, 128, 128], P('row', 'col'), may hold values from -1 to 3, as said below
- block_slots: int32 [4, 4, 4], P('row'), may hold values from 0 to 31, as said below
- offsets: int32 [4, 4, 3], P('row'), may hold values from 0 to 1792
Outputs:
- transformed: float32 [8192, 1024], P('row', 'col')
The draws below stay inside these ranges and needn't reach their ends.
Inputs may be any that keep to these rules, and one draw needn't show every extreme that they name: `wy_factors`: upper triangular; diagonal entries between 1.2 and 2.8. `block_slots`: the entries of one row group are distinct; slot k of every group lies on the col index k // 4. The border entry of the last row group is not read.
All inputs are finite; a program needn't handle non-finite values.
Results may differ from the reference program's by a relative error of at most 0.00026.
Values sent between devices are 32-bit elements; how exact they have to be, the bound alone decides.
No kernel may reach another device: no remote copies, remote signals or barrier semaphores. Data moves between devices by JAX's collectives and lax.ppermute only.
A program may use at most 64 MiB of HBM per device.

```python
import jax
import jax.numpy as jnp
from jax import lax

REFLECTOR_WIDTH = 128
REFLECTOR_ROWS = 256
ROWS_DEV = 2048
VEC_DEV = 128
STEPS = 4
BLK = 3
GROUP_SLOTS = 32
NROWS = 8192
NVEC = 1024
N_ROW = 4


def draw_block_slots(key, part):
    used = STEPS * (BLK + 1)
    group_total_count = NROWS // ROWS_DEV
    keys = jax.random.split(key, group_total_count)

    def one_group(group_sort_key, group_no):
        sorted_order = jax.random.permutation(group_sort_key, GROUP_SLOTS)
        top_position = jnp.argmax(sorted_order == GROUP_SLOTS - 1)
        rolled = jnp.roll(sorted_order, -top_position)
        chosen = jnp.where(group_no == 0, rolled, sorted_order)
        return chosen[:used]
    table = jax.vmap(one_group)(keys, jnp.arange(group_total_count))
    return table.reshape(group_total_count, STEPS, BLK + 1).astype(jnp.int32)


def draw_wy_factors(key, part):
    group_total_count = NROWS // ROWS_DEV
    first_key, second_key = jax.random.split(key)
    array_shape = (group_total_count, GROUP_SLOTS, REFLECTOR_WIDTH, REFLECTOR_WIDTH)
    diagonal = jax.random.uniform(first_key, array_shape[:3], jnp.float32, 1.5, 2.5)
    upper = 0.05 * jax.random.normal(second_key, array_shape, jnp.float32)
    strict = jnp.triu(jnp.ones((REFLECTOR_WIDTH, REFLECTOR_WIDTH), jnp.float32), 1)
    return upper * strict + diagonal[..., None] * jnp.eye(REFLECTOR_WIDTH, dtype=jnp.float32)


def plant(drawn, rng, low, largest):
    extent = drawn.shape
    index_at = [jax.random.randint(jax.random.fold_in(rng, axis), (), 0, extent[axis]) for axis in range(len(extent))]
    drawn = drawn.at[tuple(index_at)].set(low)
    longest = extent.index(max(extent))
    index_at[longest] = (index_at[longest] + 1) % extent[longest]
    return drawn.at[tuple(index_at)].set(largest)


def block_scale(rng, shape, cuts, least, largest):
    def one(dim, shards_of):
        heights = jax.random.uniform(jax.random.fold_in(jax.random.fold_in(rng, 6), dim), (shards_of,), jnp.float32, least / len(cuts), largest / len(cuts))
        return jnp.repeat(jnp.exp(heights), shape[dim] // shards_of).reshape((-1,) + (1,) * (len(shape) - dim - 1))

    level = one(*cuts[0])
    for cut in cuts[1:]:
        level = level * one(*cut)
    return level


def scatter_about(own_key, extent, deviation, bound, cuts=(), kind=jnp.bfloat16):
    loudness = block_scale(own_key, extent, cuts, -0.22, 0.18) if cuts else 1.0
    values = jax.random.normal(own_key, extent, jnp.float32) * deviation * loudness
    return jnp.minimum(jnp.maximum(values, -bound), bound).astype(kind)


def setup_inputs(seed: int = 0) -> dict:
    arg_keys = jax.random.split(jax.random.key(seed), 6)
    return {
        "vectors": scatter_about(arg_keys[0], (NROWS, NVEC), 1.0, 6.0, ((0, 4), (1, 8)), jnp.float32),
        "reflectors": scatter_about(arg_keys[1], (N_ROW, GROUP_SLOTS, REFLECTOR_ROWS, REFLECTOR_WIDTH), REFLECTOR_ROWS ** -0.5, 0.375, ((0, 4), (1, 8)), jnp.float32),
        "wy_factors": draw_wy_factors(jax.random.fold_in(arg_keys[5], 71), 0),
        "block_slots": draw_block_slots(jax.random.fold_in(arg_keys[5], 71), 0),
        "offsets": plant(jax.random.randint(arg_keys[4], (N_ROW, STEPS, BLK), 0, ROWS_DEV - REFLECTOR_ROWS + 1), jax.random.fold_in(arg_keys[4], 1), 0, ROWS_DEV - REFLECTOR_ROWS).astype(jnp.int32),
    }


def reflect(block, basis, factor):
    best = lax.Precision.HIGHEST
    coeffs = jnp.dot(basis.T, block, precision=best, preferred_element_type=jnp.float32)
    scaled = jnp.dot(factor, coeffs, precision=best, preferred_element_type=jnp.float32)
    return block - jnp.dot(basis, scaled, precision=best, preferred_element_type=jnp.float32)


def sweep(columns, reflectors, wy_factors, block_slots, offsets):
    group_total_count = NROWS // ROWS_DEV
    current = columns
    for step_no in range(STEPS):
        for group_no in range(group_total_count):
            for block_no in range(BLK + 1):
                if block_no < BLK:
                    start = (group_no * ROWS_DEV + offsets[group_no, step_no, block_no]).astype(jnp.int32)
                elif group_no < group_total_count - 1:
                    start = (group_no + 1) * ROWS_DEV - REFLECTOR_WIDTH
                else:
                    continue
                slot_id = block_slots[group_no, step_no, block_no]
                block = lax.dynamic_slice_in_dim(current, start, REFLECTOR_ROWS, 0)
                block = reflect(block, reflectors[group_no][slot_id], wy_factors[group_no][slot_id])
                current = lax.dynamic_update_slice_in_dim(current, block, start, 0)
    return current


def reference(vectors, reflectors, wy_factors, block_slots, offsets):
    pieces = vectors.reshape(NROWS, NVEC // VEC_DEV, VEC_DEV).transpose(1, 0, 2)
    result = lax.map(lambda column_set: sweep(column_set, reflectors, wy_factors, block_slots, offsets), pieces)
    return result.transpose(1, 0, 2).reshape(NROWS, NVEC)
```

```python
import functools
import math

import jax
import jax.numpy as jnp
from jax import lax
from jax.experimental import pallas as pl
from jax.experimental.pallas import tpu as pltpu
from jax.sharding import PartitionSpec as P

F32 = jnp.float32
BF16 = jnp.bfloat16


def split(x):
    high = x.astype(BF16)
    return high, (x - high.astype(F32)).astype(BF16)


def product(a, b, dims=(((1,), (0,)), ((), ()))):
    dot = functools.partial(lax.dot_general, dimension_numbers=dims, preferred_element_type=F32)
    return dot(a[0], b[0]) + (dot(a[0], b[1]) + dot(a[1], b[0]))


def ring_pairs(count, stride_of):
    return [(i, stride_of(i)) for i in range(count)]


def gather_pieces(piece, n_col, n_y):
    n_z = n_col // n_y
    me = lax.axis_index("col")
    z, y = me // n_y, me % n_y
    forward = ring_pairs(n_col, lambda i: (i + n_y) % n_col)
    backward = ring_pairs(n_col, lambda i: (i - n_y) % n_col)
    turn = ring_pairs(n_col, lambda i: i // n_y * n_y + (i % n_y + 1) % n_y)
    found = []

    def spread_y(block, dz, parts):
        sent = block
        for dy in range(1, n_y):
            sent = lax.ppermute(sent, "col", turn)
            for part, z_back in parts:
                source = (z - z_back) % n_z * n_y + (y - dy) % n_y
                found.append((sent[part], source))

    found.append((piece, me))
    count = piece.shape[0]
    low, high = piece, piece
    whole = slice(0, count)
    arrivals = [(piece, 0, [(whole, 0)])]
    for step in range(1, n_z // 2 + 1):
        if 2 * step == n_z:
            cut = count // 2
            far = jnp.concatenate(
                [lax.ppermute(low[:cut], "col", backward), lax.ppermute(high[cut:], "col", forward)], 0
            )
            found.append((far, (z - step) % n_z * n_y + y))
            arrivals.append((far, step, [(whole, step)]))
        else:
            low = lax.ppermute(low, "col", backward)
            high = lax.ppermute(high, "col", forward)
            found.append((low, (z + step) % n_z * n_y + y))
            found.append((high, (z - step) % n_z * n_y + y))
            arrivals.append((low, -step, [(whole, -step)]))
            arrivals.append((high, step, [(whole, step)]))
    for block, dz, parts in arrivals:
        spread_y(block, dz, parts)
    return found


def exchange_slots(reflectors, wy_factors, block_slots, n_col):
    hold, rows, width = reflectors.shape
    parcels = jnp.concatenate(
        [reflectors.reshape(hold, n_col, -1, width), wy_factors.reshape(hold, n_col, -1, width)], 2
    ).transpose(1, 0, 2, 3)
    parcels = lax.all_to_all(parcels, "col", 0, 0, tiled=True)
    parcels = parcels.reshape((n_col * hold,) + parcels.shape[2:])
    slots = jnp.clip(block_slots.reshape(-1), 0, n_col * hold - 1)
    return jnp.take(parcels, slots, axis=0)


def prepare_kernel(rows, width, sources, *refs):
    n = (len(refs) - 3)
    pieces, out, edge, t_scr = refs[:n], refs[n], refs[n + 1], refs[n + 2]
    v_rows, t_rows = rows // n, width // n
    per_step = out.shape[0]
    for b in range(per_step):
        for i in range(n):
            at = sources[i]
            out[b, pl.ds(pl.multiple_of(at * v_rows, v_rows), v_rows), :] = pieces[i][b, :v_rows, :]
            t_scr[b, pl.ds(pl.multiple_of(at * t_rows, t_rows), t_rows), :] = pieces[i][b, v_rows:, :]
    for b in range(per_step):
        basis = out[b, :rows, :]
        z = product(split(t_scr[b]), split(basis), (((1,), (1,)), ((), ())))
        out[b, rows : rows + width, :] = z[:, :width]
        out[b, rows + width :, :] = z[:, width:]
    edge[0, :width, :] = out[per_step - 1, width:rows, :]
    edge[0, width:, :] = out[per_step - 1, rows + width :, :]


def prepare(found, rows, width, steps):
    blocks = found[0][0].shape[0]
    per_step = blocks // steps
    n = len(found)
    v_rows, t_rows = rows // n, width // n
    if t_rows % 8:
        order = jnp.stack([source for _, source in found])
        stacked = jnp.stack([piece for piece, _ in found])
        stacked = jnp.take(stacked, jnp.argsort(order), axis=0).transpose(1, 0, 2, 3)
        found = [
            (
                jnp.concatenate(
                    [
                        stacked[:, :, :v_rows].reshape(blocks, rows, width),
                        stacked[:, :, v_rows:].reshape(blocks, width, width),
                    ],
                    1,
                ),
                jnp.int32(0),
            )
        ]
        n, v_rows, t_rows = 1, rows, width
    sources = jnp.stack([source for _, source in found]).astype(jnp.int32)
    return pl.pallas_call(
        functools.partial(prepare_kernel, rows, width),
        grid_spec=pltpu.PrefetchScalarGridSpec(
            num_scalar_prefetch=1,
            grid=(steps,),
            in_specs=[pl.BlockSpec((per_step, v_rows + t_rows, width), lambda s, _: (s, 0, 0))] * n,
            out_specs=[
                pl.BlockSpec((per_step, 2 * rows, width), lambda s, _: (s, 0, 0)),
                pl.BlockSpec((1, 2 * width, width), lambda s, _: (s, 0, 0)),
            ],
            scratch_shapes=[pltpu.VMEM((per_step, width, width), F32)],
        ),
        out_shape=[
            jax.ShapeDtypeStruct((blocks, 2 * rows, width), F32),
            jax.ShapeDtypeStruct((steps, 2 * width, width), F32),
        ],
        name="prepare",
    )(sources, *[piece for piece, _ in found])


def wave_kernel(plan, *refs):
    ticks, first, last, steps, inner, pairs, n_links = plan
    refs = list(refs)
    offs, place = refs.pop(0), refs.pop(0)
    x_in = [refs.pop(0), refs.pop(0)]
    vz = [refs.pop(0), refs.pop(0)]
    prev = [refs.pop(0), refs.pop(0)]
    if first:
        mine = [refs.pop(0) for _ in range(n_links)]
        theirs = [refs.pop(0) for _ in range(n_links)]
    x = [refs.pop(0), refs.pop(0)]
    out = refs
    p, k = place[0], place[1]
    per_step = inner + 1
    total_rows = x[0].shape[0]
    width = vz[0].shape[2]
    rows = 2 * width
    for h in range(2):
        x[h][...] = x_in[h][...]

    def valid(step):
        return (step >= 0) & (step < steps), jnp.clip(step, 0, steps - 1)

    def pick(cond, a, b):
        return jnp.where(cond, a, b)

    def down(tick):
        act, step = valid(tick - 2 * p - 1)
        block = step * per_step + inner
        is_own = k == 1
        v = pick(is_own, vz[0][block, :width, :], vz[1][block, :width, :])
        z = pick(is_own, vz[0][block, rows : rows + width, :], vz[1][block, rows : rows + width, :])
        return act & (p < pairs - 1), total_rows - width, is_own, v, z

    def up(tick):
        act, step = valid(tick - 2 * p + 1)
        v = pick(k == 0, prev[0][step, :width, :], prev[1][step, :width, :])
        z = pick(k == 0, prev[0][step, width:, :], prev[1][step, width:, :])
        return act & (p > 0), 0, k == 0, v, z

    def links(tick):
        if n_links == 2:
            return [down(tick), up(tick)]
        a, b = down(tick), up(tick)
        c = p == 0
        row = pl.multiple_of(jnp.where(c, a[1], b[1]), width)
        return [(pick(c, a[0], b[0]), row, pick(c, a[2], b[2]), pick(c, a[3], b[3]), pick(c, a[4], b[4]))]

    if first:
        for (act, row, is_own, v, _), a, b in zip(links(ticks[0] - 1), mine, theirs):
            delta = product(split(v), split(pick(act, a[...] + b[...], 0.0)))
            for h, mask in ((0, is_own), (1, jnp.logical_not(is_own))):
                at = pl.ds(row, width)
                x[h][at, :] = x[h][at, :] - pick(mask, delta, 0.0)

    for tick in ticks:
        for j in range(inner):
            for h in range(2):
                group = k if h == 0 else 1 - k
                act, step = valid(tick - 2 * p - group)
                start = offs[h, step * inner + j]
                block = step * per_step + j
                at = pl.ds(start, rows)
                xb = x[h][at, :]
                z = jnp.concatenate([vz[h][block, rows : rows + width, :], vz[h][block, rows + width :, :]], 1)
                y = pick(act, product(split(z), split(xb)), 0.0)
                x[h][at, :] = xb - product(split(vz[h][block, :rows, :]), split(y))
        if last and tick == ticks[-1]:
            for (act, row, is_own, _, z), o in zip(links(tick), out):
                at = pl.ds(row, width)
                edge = pick(is_own, x[0][at, :], x[1][at, :])
                o[...] = pick(act, product(split(z), split(edge)), 0.0)
        act, step = valid(tick - 2 * p)
        block = step * per_step + inner
        is_own = k == 0
        halves = []
        for h in range(2):
            lo, hi = (0, width) if h == 0 else (width, 0)
            v = pick(is_own, vz[0][block, lo : lo + width, :], vz[1][block, hi : hi + width, :])
            z = pick(
                is_own,
                vz[0][block, rows + lo : rows + lo + width, :],
                vz[1][block, rows + hi : rows + hi + width, :],
            )
            bottom = is_own if h == 0 else jnp.logical_not(is_own)
            row = pl.multiple_of(jnp.where(bottom, total_rows - width, 0), width)
            halves.append((v, z, pl.ds(row, width)))
        edges = [x[h][halves[h][2], :] for h in range(2)]
        y = product(split(halves[0][1]), split(edges[0])) + product(split(halves[1][1]), split(edges[1]))
        y = split(pick(act, y, 0.0))
        for h in range(2):
            x[h][halves[h][2], :] = edges[h] - product(split(halves[h][0]), y)


def wave(ticks, first, last, state, vz, prev, msgs, offs, place, steps, inner, pairs, n_links):
    plan = (tuple(ticks), first, last, steps, inner, pairs, n_links)
    vmem = pl.BlockSpec(memory_space=pltpu.VMEM)
    smem = pl.BlockSpec(memory_space=pltpu.SMEM)
    arrays = list(state) + list(vz) + list(prev) + (list(msgs[0]) + list(msgs[1]) if first else [])
    width, cols = vz[0].shape[2], state[0].shape[1]
    shapes = [jax.ShapeDtypeStruct(s.shape, F32) for s in state]
    if last:
        shapes += [jax.ShapeDtypeStruct((width, cols), F32)] * n_links
    result = pl.pallas_call(
        functools.partial(wave_kernel, plan),
        in_specs=[smem, smem] + [vmem] * len(arrays),
        out_specs=[vmem] * len(shapes),
        out_shape=shapes,
        compiler_params=pltpu.CompilerParams(vmem_limit_bytes=24 * 1024 * 1024),
        name="wave",
    )(offs, place, *arrays)
    return result[:2], result[2:]


def per_device(vectors, reflectors, wy_factors, block_slots, offsets):
    n_row, n_col = lax.axis_size("row"), lax.axis_size("col")
    pairs = n_row // 2
    row = lax.axis_index("row")
    p, k = row // 2, row % 2
    steps, inner = offsets.shape[1], offsets.shape[2]
    rows, width = reflectors.shape[2:]
    half = vectors.shape[1] // 2
    n_y = 2 ** (int(math.log2(n_col)) // 2)
    swap = [(i, i ^ 1) for i in range(n_row)]

    mine = exchange_slots(reflectors[0], wy_factors[0], block_slots[0], n_col)
    left, right = vectors[:, :half], vectors[:, half:]
    own = jnp.where(k == 0, left, right)
    other = lax.ppermute(jnp.where(k == 0, right, left), "row", swap)
    offs_own = offsets[0].reshape(-1)
    offs_other = lax.ppermute(offs_own, "row", swap)
    offs = jnp.clip(jnp.stack([offs_own, offs_other]), 0, vectors.shape[0] - rows)
    place = jnp.stack([p, k]).astype(jnp.int32)

    found = gather_pieces(mine, n_col, n_y)
    vz_own, edge = prepare(found, rows, width, steps)
    vz_other = lax.ppermute(vz_own, "row", swap)
    above = lax.ppermute(edge, "row", [(i, i + 1) for i in range(1, n_row - 1, 2)])
    above_again = lax.ppermute(above, "row", [(i, i + 1) for i in range(0, n_row, 2)])

    n_links = 1 if pairs == 2 else 2
    last_tick = n_row + steps - 2
    stops = [
        t
        for t in range(last_tick + 1)
        if any(0 <= t - 2 * q - 1 < steps for q in range(pairs - 1))
    ]
    state, msgs, first, ticks = (own, other), None, False, []
    for t in range(last_tick + 1):
        ticks.append(t)
        last = t in stops
        if not last and t < last_tick:
            continue
        state, sent = wave(
            ticks, first, last, state, (vz_own, vz_other), (above, above_again), msgs, offs, place,
            steps, inner, pairs, n_links,
        )
        if last:
            if n_links == 1:
                got = [lax.ppermute(sent[0], "row", [(i, (i + 2) % 4) for i in range(4)])]
            else:
                got = [
                    lax.ppermute(sent[1], "row", [(i + 2, i) for i in range(n_row - 2)]),
                    lax.ppermute(sent[0], "row", [(i, i + 2) for i in range(n_row - 2)]),
                ]
            msgs = (sent, got)
        first, ticks = last, []
    own, other = state
    back = lax.ppermute(other, "row", swap)
    return jnp.where(k == 0, jnp.concatenate([own, back], 1), jnp.concatenate([back, own], 1))


def solution(mesh):
    in_specs = (
        P("row", "col"),
        P("row", "col", None, None),
        P("row", "col", None, None),
        P("row", None, None),
        P("row", None, None),
    )
    out_specs = P("row", "col")
    return jax.shard_map(
        per_device, mesh=mesh, in_specs=in_specs, out_specs=out_specs, check_vma=False
    )
```
